32 devices in a mesh: segment: 2 (over x), expert: 16 (over z, y, core).
Axes of the slice: x: 2, y: 2, z: 4, core: 2. Of those that a mesh axis runs over, the one named last changes fastest.
Arguments:
- fwd_acts: bfloat16 [2, 384, 2048], P('segment', 'expert'), may hold values from -6 to 6
- fwd_ids: int32 [2, 384, 8], P('segment', 'expert'), may hold values from 0 to 15, all different within a row; in each aligned block of 24 rows (0 to 23, 24 to 47, ..., all dimensions but the last counted through in order) at most 12 rows name the same one
- fwd_prob: float32 [2, 384, 8], P('segment', 'expert'), may hold values from 0.02 to 0.3
- bwd_acts: bfloat16 [2, 384, 2048], P('segment', 'expert'), may hold values from -6 to 6
- bwd_ids: int32 [2, 384, 8], P('segment', 'expert'), may hold values from 0 to 15, all different within a row; in each aligned block of 24 rows (0 to 23, 24 to 47, ..., all dimensions but the last counted through in order) at most 12 rows name the same one
- bwd_prob: float32 [2, 384, 8], P('segment', 'expert'), may hold values from 0.02 to 0.3
- grad_in: bfloat16 [2, 384, 2048], P('segment', 'expert'), may hold values from -6 to 6
- w_gate: bfloat16 [2, 16, 2048, 384], P('segment', 'expert'), may hold values from -0.125 to 0.125
- w_up: bfloat16 [2, 16, 2048, 384], P('segment', 'expert'), may hold values from -0.125 to 0.125
- w_down: bfloat16 [2, 16, 384, 2048], P('segment', 'expert'), may hold values from -0.3125 to 0.3125
Outputs:
- fwd_out: bfloat16 [2, 384, 2048], P('segment', 'expert')
- bwd_out: bfloat16 [2, 384, 2048], P('segment', 'expert')
The draws below stay inside these ranges and needn't reach their ends.
Inputs may be any that keep to these rules, and one draw needn't show every extreme that they name: `fwd_ids`: each token names 8 different experts. Among the 24 tokens of one block no expert is named by more than 12 tokens, and in every draw some expert is named by exactly 12 tokens of a block. `bwd_ids`: as for fwd_ids.
All inputs are finite; a program needn't handle non-finite values.
Results may differ from the reference program's by a relative error of at most 0.0064.
Values may be sent and summed in bfloat16 or wider, within the bound.
A program may use at most 64 MiB of HBM per device.

```python
import math
import jax
import jax.numpy as jnp
import numpy as np
from jax import lax

D = 2048
TOP = 8
HIDDEN_SIZE = 384
TOK_DEV = 24
EXPERTS = 16
SEGMENTS = 2
TOKENS = 384
CAP = 12
N_EXPERT = 16


def levels(stream_key, extent, cuts, least, top_value):
    def one(position, blocks):
        steps = jax.random.uniform(jax.random.fold_in(jax.random.fold_in(stream_key, 6), position), (blocks,), jnp.float32, least / len(cuts), top_value / len(cuts))
        return jnp.repeat(jnp.exp(steps), extent[position] // blocks).reshape((-1,) + (1,) * (len(extent) - position - 1))

    factor_of = one(*cuts[0])
    for cut in cuts[1:]:
        factor_of = factor_of * one(*cut)
    return factor_of


def assign_block(own_key, own, number, rows, number_of, top, reach, skew):
    sequence = jax.random.permutation(own_key, number_of)
    heavy_load, common = portions_of(number_of, rows * top, reach, skew, True), portions_of(number_of, rows * top, reach, skew, False)
    places = jnp.arange(number_of)

    def named(sizes, rotation):
        used = int((sizes > 0).sum())
        fixed = max(1, used // 4)
        shifted = fixed + (places - fixed + rotation * (used - fixed)) % max(1, number_of - fixed)
        return jnp.zeros((number_of,), jnp.int32).at[sequence[jnp.where(places < fixed, places, shifted)]].set(jnp.asarray(sizes, jnp.int32))

    sizes = jnp.where(number % 4 == 0, named(heavy_load, number // 4), named(common, number - number // 4 - 1))
    mixed = jax.random.permutation(jax.random.fold_in(own, 3), number_of)
    source_of, taker = mixed[0:number_of // 2 * 2:2], mixed[1:number_of // 2 * 2:2]
    margin = jnp.minimum(sizes[source_of] - 1, reach - sizes[taker]) // 2
    margin = jnp.where((source_of == sequence[0]) | (taker == sequence[0]) | (sizes[taker] == 0), 0, jnp.maximum(margin, 0))
    shifted = jax.random.randint(jax.random.fold_in(own, 4), (number_of // 2,), 0, 1 << 20) % (margin + 1)
    sizes = sizes.at[source_of].add(-shifted).at[taker].add(shifted)
    members = jnp.searchsorted(jnp.cumsum(sizes), jnp.arange(rows * top), side="right").astype(jnp.int32)
    listing = members.reshape(top, rows).T
    listing = listing[jax.random.permutation(jax.random.fold_in(own, 1), rows)]
    rotation = jax.random.randint(jax.random.fold_in(own, 2), (rows, 1), 0, top)
    return jnp.take_along_axis(listing, (jnp.arange(top)[None, :] + rotation) % top, axis=1)


def portions_of(number_of, total, limit, lean, full):
    portions = [(1 << 20) // math.isqrt(grade ** lean) + 1 for grade in range(1, number_of + 1)]
    largest = limit if full else min(limit, max(-(-total // number_of), total * portions[0] // sum(portions)))
    least = 1 if total - largest >= number_of - 1 else 0
    counts, rest = [largest] + [least] * (number_of - 1), total - largest - least * (number_of - 1)
    while rest > 0:
        free = [i for i in range(1, number_of) if counts[i] < largest] or [i for i in range(1, number_of) if counts[i] < limit]
        whole, budget = sum([portions[i] for i in free]), rest
        for i in free:
            more = min(limit - counts[i], max(1, budget * portions[i] // whole), rest)
            counts[i] = counts[i] + more
            rest = rest - more
    return np.array(counts)


def bell_draw(own_key, extent, scale, most, split=(), kind=jnp.bfloat16):
    values = scale * jax.random.normal(own_key, extent, jnp.float32)
    if split:
        values = values * levels(own_key, extent, split, -0.22, 0.18)
    return jnp.clip(values, -most, most).astype(kind)


def setup_inputs(seed: int = 0) -> dict:
    keys = jax.random.split(jax.random.key(seed), 11)
    fwd_acts = bell_draw(keys[0], (SEGMENTS, TOKENS, D), 1.0, 6.0, ((0, 2), (1, 16)))
    fwd_ids_keys = jax.random.split(jax.random.fold_in(keys[1], 1), SEGMENTS * TOKENS // TOK_DEV)
    fwd_ids_turns = jax.random.permutation(jax.random.fold_in(keys[1], 3), SEGMENTS * TOKENS // TOK_DEV)
    fwd_ids = jax.vmap(lambda own, number: assign_block(jax.random.fold_in(keys[1], 2), own, number, TOK_DEV, EXPERTS, TOP, CAP, 2))(fwd_ids_keys, fwd_ids_turns).reshape((SEGMENTS, TOKENS, TOP))
    fwd_prob = jnp.clip(0.02 + 0.28 * jax.random.uniform(keys[2], (SEGMENTS, TOKENS, TOP), jnp.float32) ** levels(keys[2], (SEGMENTS, TOKENS, TOP), ((0, 2), (1, 16)), -0.2, 0.2), 0.02, 0.3)
    bwd_acts = bell_draw(keys[3], (SEGMENTS, TOKENS, D), 1.0, 6.0, ((0, 2), (1, 16)))
    bwd_ids_keys = jax.random.split(jax.random.fold_in(keys[4], 1), SEGMENTS * TOKENS // TOK_DEV)
    bwd_ids_turns = jax.random.permutation(jax.random.fold_in(keys[4], 3), SEGMENTS * TOKENS // TOK_DEV)
    bwd_ids = jax.vmap(lambda own, number: assign_block(jax.random.fold_in(keys[4], 2), own, number, TOK_DEV, EXPERTS, TOP, CAP, 2))(bwd_ids_keys, bwd_ids_turns).reshape((SEGMENTS, TOKENS, TOP))
    bwd_prob = jnp.clip(0.02 + 0.28 * jax.random.uniform(keys[5], (SEGMENTS, TOKENS, TOP), jnp.float32) ** levels(keys[5], (SEGMENTS, TOKENS, TOP), ((0, 2), (1, 16)), -0.2, 0.2), 0.02, 0.3)
    grad_in = bell_draw(keys[6], (SEGMENTS, TOKENS, D), 1.0, 6.0, ((0, 2), (1, 16)))
    w_gate = bell_draw(keys[7], (SEGMENTS, EXPERTS, D, HIDDEN_SIZE), D ** -0.5, 0.125, ((0, 2), (1, 16)))
    w_up = bell_draw(keys[8], (SEGMENTS, EXPERTS, D, HIDDEN_SIZE), D ** -0.5, 0.125, ((0, 2), (1, 16)))
    w_down = bell_draw(keys[9], (SEGMENTS, EXPERTS, HIDDEN_SIZE, D), HIDDEN_SIZE ** -0.5, 0.3125, ((0, 2), (1, 16)))
    return dict(fwd_acts=fwd_acts, fwd_ids=fwd_ids, fwd_prob=fwd_prob, bwd_acts=bwd_acts, bwd_ids=bwd_ids, bwd_prob=bwd_prob, grad_in=grad_in, w_gate=w_gate, w_up=w_up, w_down=w_down)


def routing(expert_ids, gate_prob, experts, capacity):
    tok_count = expert_ids.shape[0]
    pick_count = expert_ids.shape[1]
    entry_count = tok_count * pick_count
    flat_ids = expert_ids.reshape(entry_count)
    one_hot = (flat_ids[:, None] == jnp.arange(experts, dtype=jnp.int32)[None, :]).astype(jnp.float32)
    entry_index = jnp.arange(entry_count, dtype=jnp.int32)
    strictly_lower = (entry_index[:, None] > entry_index[None, :]).astype(jnp.float32)
    earlier = jnp.dot(strictly_lower, one_hot, precision=lax.Precision.HIGHEST)
    slot_index = jnp.sum(earlier * one_hot, axis=1)
    slot_range = jnp.arange(capacity, dtype=jnp.int32).astype(jnp.float32)
    slot_hot = (slot_range[None, :] == slot_index[:, None]).astype(jnp.float32)
    placed = (one_hot[:, :, None] * slot_hot[:, None, :]).reshape(tok_count, pick_count, experts * capacity)
    select_mat = jnp.sum(placed, axis=1)
    weigh_mat = jnp.sum(placed * gate_prob.astype(jnp.float32)[:, :, None], axis=1)
    return select_mat, weigh_mat


def dispatch(select_mat, values):
    moved = lax.dot_general(select_mat.astype(jnp.bfloat16), values, (((0,), (0,)), ((), ())), preferred_element_type=jnp.float32)
    return moved.astype(jnp.bfloat16)


def weigh_rows(weigh_mat, grads):
    moved = lax.dot_general(weigh_mat, grads.astype(jnp.float32), (((0,), (0,)), ((), ())), precision=lax.Precision.HIGHEST, preferred_element_type=jnp.float32)
    return moved.astype(jnp.bfloat16)


def collect(matrix, rows):
    return jnp.dot(matrix, rows.astype(jnp.float32), precision=lax.Precision.HIGHEST).astype(jnp.bfloat16)


def expert_forward(rows, gate_mat, up_mat, down_mat):
    gate_pre = jnp.dot(rows, gate_mat, preferred_element_type=jnp.float32)
    up_pre = jnp.dot(rows, up_mat, preferred_element_type=jnp.float32)
    hidden = (jax.nn.silu(gate_pre) * up_pre).astype(jnp.bfloat16)
    return jnp.dot(hidden, down_mat, preferred_element_type=jnp.float32).astype(jnp.bfloat16)


def expert_backward(rows, grad_rows, gate_mat, up_mat, down_mat):
    contract = (((1,), (1,)), ((), ()))
    gate_pre = jnp.dot(rows, gate_mat, preferred_element_type=jnp.float32)
    up_pre = jnp.dot(rows, up_mat, preferred_element_type=jnp.float32)
    grad_hidden = lax.dot_general(grad_rows, down_mat, contract, preferred_element_type=jnp.float32)
    sigma = jax.nn.sigmoid(gate_pre)
    grad_gate = (grad_hidden * up_pre * sigma * (1.0 + gate_pre * (1.0 - sigma))).astype(jnp.bfloat16)
    grad_up = (grad_hidden * gate_pre * sigma).astype(jnp.bfloat16)
    back = lax.dot_general(grad_gate, gate_mat, contract, preferred_element_type=jnp.float32)
    back = back + lax.dot_general(grad_up, up_mat, contract, preferred_element_type=jnp.float32)
    return back.astype(jnp.bfloat16)


def to_experts(buffers):
    return buffers.reshape(N_EXPERT, EXPERTS, CAP, D).transpose(1, 0, 2, 3).reshape(EXPERTS, N_EXPERT * CAP, D)


def from_experts(rows):
    return rows.reshape(EXPERTS, N_EXPERT, CAP, D).transpose(1, 0, 2, 3).reshape(N_EXPERT, EXPERTS * CAP, D)


def block_routing(expert_ids, gate_prob):
    def one_block(ids_block, prob_block):
        return routing(ids_block, prob_block, EXPERTS, CAP)

    return jax.vmap(one_block)(expert_ids.reshape(N_EXPERT, TOK_DEV, TOP), gate_prob.reshape(N_EXPERT, TOK_DEV, TOP))


def forward_section(packed):
    acts, expert_ids, gate_prob, gate_all, up_all, down_all = packed
    select_mat, weigh_mat = block_routing(expert_ids, gate_prob)
    sent = jax.vmap(dispatch)(select_mat, acts.reshape(N_EXPERT, TOK_DEV, D))

    def one_expert(item):
        return expert_forward(item[0], item[1], item[2], item[3])

    outputs = lax.map(one_expert, (to_experts(sent), gate_all, up_all, down_all))
    return jax.vmap(collect)(weigh_mat, from_experts(outputs)).reshape(TOKENS, D)


def backward_section(packed):
    acts, expert_ids, gate_prob, grads, gate_all, up_all, down_all = packed
    select_mat, weigh_mat = block_routing(expert_ids, gate_prob)
    sent = jax.vmap(dispatch)(select_mat, acts.reshape(N_EXPERT, TOK_DEV, D))
    grads_sent = jax.vmap(weigh_rows)(weigh_mat, grads.reshape(N_EXPERT, TOK_DEV, D))

    def one_expert(item):
        return expert_backward(item[0], item[1], item[2], item[3], item[4])

    outputs = lax.map(one_expert, (to_experts(sent), to_experts(grads_sent), gate_all, up_all, down_all))
    return jax.vmap(collect)(select_mat, from_experts(outputs)).reshape(TOKENS, D)


def reference(fwd_acts, fwd_ids, fwd_prob, bwd_acts, bwd_ids, bwd_prob, grad_in, w_gate, w_up, w_down):
    forward = lax.map(forward_section, (fwd_acts, fwd_ids, fwd_prob, w_gate, w_up, w_down))
    backward = lax.map(backward_section, (bwd_acts, bwd_ids, bwd_prob, grad_in, w_gate, w_up, w_down))
    return jnp.roll(forward, 1, axis=0), jnp.roll(backward, -1, axis=0)
```

```python
import functools

import jax
import jax.numpy as jnp
from jax import lax
from jax.experimental import pallas as pl
from jax.experimental.pallas import tpu as pltpu
from jax.sharding import PartitionSpec as P

TOP = 8


def shifted(array, axis, by):
    count = lax.axis_size(axis)
    return lax.ppermute(array, axis, [(i, (i + by) % count) for i in range(count)])


def routing(expert_ids, gate_prob, experts, capacity):
    tok_count = expert_ids.shape[0]
    pick_count = expert_ids.shape[1]
    entry_count = tok_count * pick_count
    flat_ids = expert_ids.reshape(entry_count)
    one_hot = (flat_ids[:, None] == jnp.arange(experts, dtype=jnp.int32)[None, :]).astype(
        jnp.float32
    )
    entry_index = jnp.arange(entry_count, dtype=jnp.int32)
    strictly_lower = (entry_index[:, None] > entry_index[None, :]).astype(jnp.float32)
    earlier = jnp.dot(strictly_lower, one_hot, precision=lax.Precision.HIGHEST)
    slot_index = jnp.sum(earlier * one_hot, axis=1)
    slot_range = jnp.arange(capacity, dtype=jnp.int32).astype(jnp.float32)
    slot_hot = (slot_range[None, :] == slot_index[:, None]).astype(jnp.float32)
    placed = (one_hot[:, :, None] * slot_hot[:, None, :]).reshape(
        tok_count, pick_count, experts * capacity
    )
    select_mat = jnp.sum(placed, axis=1)
    weigh_mat = jnp.sum(placed * gate_prob[:, :, None], axis=1)
    return (select_mat, weigh_mat)


def dispatch(select_mat, values):
    moved = lax.dot_general(
        select_mat.astype(jnp.bfloat16),
        values,
        (((0,), (0,)), ((), ())),
        preferred_element_type=jnp.float32,
    )
    return moved.astype(jnp.bfloat16)


def weigh_rows(weigh_mat, grads):
    moved = lax.dot_general(
        weigh_mat,
        grads.astype(jnp.float32),
        (((0,), (0,)), ((), ())),
        precision=lax.Precision.HIGHEST,
        preferred_element_type=jnp.float32,
    )
    return moved.astype(jnp.bfloat16)


def collect(matrix, rows):
    return jnp.dot(matrix, rows.astype(jnp.float32), precision=lax.Precision.HIGHEST).astype(
        jnp.bfloat16
    )


def expert_forward(rows, gate_mat, up_mat, down_mat):
    gate_pre = jnp.dot(rows, gate_mat, preferred_element_type=jnp.float32)
    up_pre = jnp.dot(rows, up_mat, preferred_element_type=jnp.float32)
    hidden = (jax.nn.silu(gate_pre) * up_pre).astype(jnp.bfloat16)
    return jnp.dot(hidden, down_mat, preferred_element_type=jnp.float32).astype(jnp.bfloat16)


def expert_backward(rows, grad_rows, gate_mat, up_mat, down_mat):
    contract = (((1,), (1,)), ((), ()))
    gate_pre = jnp.dot(rows, gate_mat, preferred_element_type=jnp.float32)
    up_pre = jnp.dot(rows, up_mat, preferred_element_type=jnp.float32)
    grad_hidden = lax.dot_general(grad_rows, down_mat, contract, preferred_element_type=jnp.float32)
    sigma = jax.nn.sigmoid(gate_pre)
    grad_gate = (grad_hidden * up_pre * sigma * (1.0 + gate_pre * (1.0 - sigma))).astype(
        jnp.bfloat16
    )
    grad_up = (grad_hidden * gate_pre * sigma).astype(jnp.bfloat16)
    back = lax.dot_general(grad_gate, gate_mat, contract, preferred_element_type=jnp.float32)
    back = back + lax.dot_general(grad_up, up_mat, contract, preferred_element_type=jnp.float32)
    return back.astype(jnp.bfloat16)


def plain_body(fwd_acts, fwd_ids, fwd_prob, bwd_acts, bwd_ids, bwd_prob, grad_in, w_gate, w_up, w_down):
    experts = lax.axis_size("expert")
    tok_count = fwd_acts.shape[1]
    width = fwd_acts.shape[2]
    capacity = max(2, (tok_count * TOP + experts - 1) // experts)
    gate_mat = w_gate[0, 0]
    up_mat = w_up[0, 0]
    down_mat = w_down[0, 0]
    fwd_select, fwd_weigh = routing(fwd_ids[0], fwd_prob[0], experts, capacity)
    bwd_select, bwd_weigh = routing(bwd_ids[0], bwd_prob[0], experts, capacity)
    fwd_rows = dispatch(fwd_select, fwd_acts[0]).reshape(experts, capacity, width)
    bwd_rows = dispatch(bwd_select, bwd_acts[0]).reshape(experts, capacity, width)
    grad_rows = weigh_rows(bwd_weigh, grad_in[0]).reshape(experts, capacity, width)

    def backward_rows(received, received_grad):
        flat_grad = received_grad.reshape(-1, width)
        return expert_backward(
            received.reshape(-1, width), flat_grad, gate_mat, up_mat, down_mat
        ).reshape(received.shape)

    received = lax.all_to_all(fwd_rows, "expert", split_axis=0, concat_axis=0, tiled=True)
    fwd_back = lax.all_to_all(
        expert_forward(received.reshape(-1, width), gate_mat, up_mat, down_mat).reshape(
            received.shape
        ),
        "expert",
        split_axis=0,
        concat_axis=0,
        tiled=True,
    )
    received = (
        lax.all_to_all(bwd_rows, "expert", split_axis=0, concat_axis=0, tiled=True),
        lax.all_to_all(grad_rows, "expert", split_axis=0, concat_axis=0, tiled=True),
    )
    bwd_back = lax.all_to_all(
        backward_rows(received[0], received[1]), "expert", split_axis=0, concat_axis=0, tiled=True
    )
    fwd_result = collect(fwd_weigh, fwd_back.reshape(-1, width))
    bwd_result = collect(bwd_select, bwd_back.reshape(-1, width))
    fwd_out = shifted(fwd_result[None], "segment", 1)
    bwd_out = shifted(bwd_result[None], "segment", -1)
    return (fwd_out, bwd_out)


MESH = pl.DeviceIdType.MESH
LANES = 128
NT = (((1,), (1,)), ((), ()))
BWD, GRAD, FWD = 0, 1, 2


def moe_kernel(
    n,
    sections,
    chunks,
    bwd_ref,
    grad_ref,
    fwd_ref,
    fid_ref,
    fpr_ref,
    bid_ref,
    bpr_ref,
    wg_ref,
    wu_ref,
    wd_ref,
    fout_ref,
    bout_ref,
    gat,
    prob,
    xbuf,
    gbuf,
    wgate,
    wup,
    wdown,
    part,
    mid,
    own,
    ysend,
    yrecv,
    zsend,
    zrecv,
    local_sem,
    wlocal_sem,
    wsend_sem,
    wrecv_sem,
    az_send,
    az_recv,
    ay_send,
    ay_recv,
    ry_send,
    ry_recv,
    rz_send,
    rz_recv,
):
    far = n // 4
    tok, width = bwd_ref.shape
    hid = wd_ref.shape[0]
    rows = 2 * far * tok
    cw = width // chunks
    sec = lax.axis_index("segment")
    me = lax.axis_index("expert")
    core = lax.rem(me, 2)
    y = lax.rem(me // 2, 2)
    z = me // 4

    def place(zz, yy, cc):
        return (zz * 2 + yy) * 2 + cc

    partner = place(z, y, 1 - core)
    across = place(z, 1 - y, core)
    next_sec = lax.rem(sec + 1, sections)
    prev_sec = lax.rem(sec + sections - 1, sections)
    peers = [lax.rem(z + d, far) for d in range(1, far)]

    barrier = pltpu.get_barrier_semaphore()
    greeted = [(sec, partner), (sec, across)] + [(sec, place(p, y, core)) for p in peers]
    for other in [next_sec] if sections == 2 else [next_sec, prev_sec]:
        greeted += [(other, place(zz, y, core)) for zz in range(far)]
    for target in greeted:
        pl.semaphore_signal(barrier, inc=1, device_id=target, device_id_type=MESH)

    local = []
    for a, ref in ((BWD, bwd_ref), (GRAD, grad_ref), (FWD, fwd_ref)):
        local.append(pltpu.make_async_copy(ref, gat.at[a, 0, z], local_sem.at[a]))
    for cp in local:
        cp.start()
    wlocal = [
        pltpu.make_async_copy(ref, buf.at[0], wlocal_sem.at[k])
        for k, (ref, buf) in enumerate(((wg_ref, wgate), (wu_ref, wup), (wd_ref, wdown)))
    ]
    for cp in wlocal:
        cp.start()
    lanes = prob.shape[-1]
    lane = lax.broadcasted_iota(jnp.int32, (tok, lanes), 1)
    table = jnp.zeros((tok, lanes), jnp.float32)
    for k in range(fid_ref.shape[1]):
        table += jnp.where(fid_ref[:, k : k + 1] == lane, fpr_ref[:, k : k + 1], 0.0)
        table += jnp.where(bid_ref[:, k : k + 1] + n == lane, bpr_ref[:, k : k + 1], 0.0)
    prob[0, z] = table

    pl.semaphore_wait(barrier, len(greeted))

    def view(a):
        return prob if a == 3 else gat.at[a]

    def remote(src, dst, send, recv, device):
        return pltpu.make_async_remote_copy(
            src_ref=src,
            dst_ref=dst,
            send_sem=send,
            recv_sem=recv,
            device_id=device,
            device_id_type=MESH,
        )

    def z_copy(a, src, k, p):
        return remote(
            src, view(a).at[0, z], az_send.at[a, k], az_recv.at[a, z], (sec, place(p, y, core))
        )

    def y_copy(a, src, zs):
        return remote(src, view(a).at[1, zs], ay_send.at[a, zs], ay_recv.at[a, zs], (sec, across))

    started = []
    for a, ref in ((BWD, bwd_ref), (GRAD, grad_ref), (3, prob.at[0, z]), (FWD, fwd_ref)):
        for k, p in enumerate(peers):
            cp = z_copy(a, ref, k, p)
            cp.start()
            started.append(cp)
        cp = y_copy(a, ref, z)
        cp.start()
        started.append(cp)
        if a == BWD:
            for k, (w, buf) in enumerate(((wg_ref, wgate), (wu_ref, wup), (wd_ref, wdown))):
                cp = remote(
                    w, buf.at[1], wsend_sem.at[k], wrecv_sem.at[k], (sec, partner)
                )
                cp.start()
                started.append(cp)

    def forward_rows(a):
        for d in range(1, far):
            zs = lax.rem(z + far - d, far)
            ref = view(a).at[0, zs]
            remote(ref, ref, az_send.at[a, 0], az_recv.at[a, zs], (sec, across)).wait_recv()
            cp = y_copy(a, ref, zs)
            cp.start()
            started.append(cp)

    def arrive(a):
        for zs in range(far):
            ref = view(a).at[1, zs]
            remote(ref, ref, ay_send.at[a, zs], ay_recv.at[a, zs], (sec, across)).wait_recv()

    def flatten(a, dst):
        for b in range(far):
            both = []
            for q in (2 * b, 2 * b + 1):
                both.append(gat[a, q // far, q % far].astype(jnp.float32))
            dst[2 * b * tok : (2 * b + 2) * tok, :] = jnp.concatenate(both, axis=0).astype(
                jnp.bfloat16
            )

    def weight_of(base, slot):
        index = base + (me if slot == 0 else partner)
        full = prob[...].reshape(rows, lanes)
        at = lax.broadcasted_iota(jnp.int32, (rows, lanes), 1) == index
        return jnp.sum(jnp.where(at, full, 0.0), axis=1, keepdims=True)

    def partial_out(r, c, value):
        half = far * tok
        own[r, c] = value[:half]
        for zz in range(far):
            lo = half + zz * tok
            ysend[r, c, zz] = value[lo : lo + tok].astype(jnp.bfloat16)
        cp = remote(
            ysend.at[r, c], yrecv.at[r, c], ry_send.at[r, c], ry_recv.at[r, c], (sec, across)
        )
        cp.start()
        started.append(cp)

    def second_hop(r, section):
        for c in range(chunks):
            remote(
                ysend.at[r, c], yrecv.at[r, c], ry_send.at[r, c], ry_recv.at[r, c], (sec, across)
            ).wait_recv()
            for zz in range(far):
                total = own[r, c, zz * tok : (zz + 1) * tok] + yrecv[r, c, zz].astype(jnp.float32)
                zsend[r, c, zz] = total.astype(jnp.bfloat16)
            for zz in range(far):
                cp = remote(
                    zsend.at[r, c, zz],
                    zrecv.at[r, c, z],
                    rz_send.at[r, c, zz],
                    rz_recv.at[r, c, z],
                    (section, place(zz, y, core)),
                )
                cp.start()
                started.append(cp)

    def finish(r, section, out_ref):
        for c in range(chunks):
            total = None
            for zz in range(far):
                ref = zrecv.at[r, c, zz]
                remote(
                    ref, ref, rz_send.at[r, c, zz], rz_recv.at[r, c, zz], (section, me)
                ).wait_recv()
                got = zrecv[r, c, zz].astype(jnp.float32)
                total = got if total is None else total + got
            out_ref[:, c * cw : (c + 1) * cw] = total.astype(jnp.bfloat16)

    def mm(a, b):
        return jnp.dot(a, b, preferred_element_type=jnp.float32)

    def mm_t(a, b):
        return lax.dot_general(a, b, NT, preferred_element_type=jnp.float32)

    forward_rows(BWD)
    forward_rows(GRAD)
    forward_rows(3)
    local[BWD].wait()
    arrive(BWD)
    flatten(BWD, xbuf)
    for slot in range(2):
        for k in range(3):
            if slot == 0:
                wlocal[k].wait()
            else:
                buf = (wgate, wup, wdown)[k].at[1]
                remote(buf, buf, wsend_sem.at[k], wrecv_sem.at[k], (sec, partner)).wait_recv()
        part[0] = mm(xbuf[...], wgate[slot])
        part[1] = mm(xbuf[...], wup[slot])
        if slot == 0:
            local[GRAD].wait()
            arrive(GRAD)
            arrive(3)
            flatten(GRAD, gbuf)
        grad_hidden = mm_t(gbuf[...], wdown[slot]) * weight_of(n, slot)
        gate_pre = part[0]
        sigma = jax.nn.sigmoid(gate_pre)
        mid[2 * slot] = (
            grad_hidden * part[1] * sigma * (1.0 + gate_pre * (1.0 - sigma))
        ).astype(jnp.bfloat16)
        mid[2 * slot + 1] = (grad_hidden * gate_pre * sigma).astype(jnp.bfloat16)
        if slot == 0:
            forward_rows(FWD)
    for c in range(chunks):
        cols = slice(c * cw, (c + 1) * cw)
        value = mm_t(mid[0], wgate[0, cols, :])
        value += mm_t(mid[1], wup[0, cols, :])
        value += mm_t(mid[2], wgate[1, cols, :])
        value += mm_t(mid[3], wup[1, cols, :])
        partial_out(0, c, value)

    local[FWD].wait()
    arrive(FWD)
    flatten(FWD, xbuf)
    for slot in range(2):
        part[0] = mm(xbuf[...], wgate[slot])
        up_pre = mm(xbuf[...], wup[slot])
        gate_pre = part[0]
        hidden = gate_pre * jax.nn.sigmoid(gate_pre) * up_pre * weight_of(0, slot)
        mid[slot] = hidden.astype(jnp.bfloat16)
        if slot == 0:
            second_hop(0, prev_sec)
    for c in range(chunks):
        cols = slice(c * cw, (c + 1) * cw)
        value = mm(mid[0], wdown[0, :, cols])
        value += mm(mid[1], wdown[1, :, cols])
        partial_out(1, c, value)
    second_hop(1, next_sec)
    finish(0, prev_sec, bout_ref)
    finish(1, next_sec, fout_ref)
    for cp in started:
        cp.wait_send()


def fused_body(n, sections, chunks, *args):
    fwd_acts, fwd_ids, fwd_prob, bwd_acts, bwd_ids, bwd_prob, grad_in, w_gate, w_up, w_down = args
    tok, width = fwd_acts.shape[1:]
    hid = w_down.shape[2]
    far = n // 4
    rows = 2 * far * tok
    cw = width // chunks
    lanes = -(-2 * n // LANES) * LANES
    bf, f32 = jnp.bfloat16, jnp.float32
    dma = pltpu.SemaphoreType.DMA
    fwd_out, bwd_out = pl.pallas_call(
        functools.partial(moe_kernel, n, sections, chunks),
        out_shape=[jax.ShapeDtypeStruct((tok, width), bf)] * 2,
        in_specs=[pl.BlockSpec(memory_space=pl.ANY)] * 3
        + [pl.BlockSpec(memory_space=pltpu.VMEM)] * 4
        + [pl.BlockSpec(memory_space=pl.ANY)] * 3,
        out_specs=[pl.BlockSpec(memory_space=pltpu.VMEM)] * 2,
        scratch_shapes=[
            pltpu.VMEM((3, 2, far, tok, width), bf),
            pltpu.VMEM((2, far, tok, lanes), f32),
            pltpu.VMEM((rows, width), bf),
            pltpu.VMEM((rows, width), bf),
            pltpu.VMEM((2, width, hid), bf),
            pltpu.VMEM((2, width, hid), bf),
            pltpu.VMEM((2, hid, width), bf),
            pltpu.VMEM((2, rows, hid), f32),
            pltpu.VMEM((4, rows, hid), bf),
            pltpu.VMEM((2, chunks, far * tok, cw), f32),
            pltpu.VMEM((2, chunks, far, tok, cw), bf),
            pltpu.VMEM((2, chunks, far, tok, cw), bf),
            pltpu.VMEM((2, chunks, far, tok, cw), bf),
            pltpu.VMEM((2, chunks, far, tok, cw), bf),
            dma((3,)),
            dma((3,)),
            dma((3,)),
            dma((3,)),
            dma((4, far)),
            dma((4, far)),
            dma((4, far)),
            dma((4, far)),
            dma((2, chunks)),
            dma((2, chunks)),
            dma((2, chunks, far)),
            dma((2, chunks, far)),
        ],
        compiler_params=pltpu.CompilerParams(
            collective_id=0, has_side_effects=True, vmem_limit_bytes=60 * 1024 * 1024
        ),
    )(
        bwd_acts[0],
        grad_in[0],
        fwd_acts[0],
        fwd_ids[0],
        fwd_prob[0],
        bwd_ids[0],
        bwd_prob[0],
        w_gate[0, 0],
        w_up[0, 0],
        w_down[0, 0],
    )
    return fwd_out[None], bwd_out[None]


def body(*args):
    n = lax.axis_size("expert")
    sections = lax.axis_size("segment")
    tok, width = args[0].shape[1:]
    gathered = n * tok * width * 2
    fits = n % 4 == 0 and n >= 8 and sections > 1 and tok % 8 == 0 and width % 512 == 0
    if not fits or gathered > 4 * 1024 * 1024:
        return plain_body(*args)
    return fused_body(n, sections, width // 512, *args)


def solution(mesh):
    return jax.shard_map(
        body,
        mesh=mesh,
        in_specs=(
            P("segment", "expert", None),
            P("segment", "expert", None),
            P("segment", "expert", None),
            P("segment", "expert", None),
            P("segment", "expert", None),
            P("segment", "expert", None),
            P("segment", "expert", None),
            P("segment", "expert", None, None),
            P("segment", "expert", None, None),
            P("segment", "expert", None, None),
        ),
        out_specs=(P("segment", "expert", None), P("segment", "expert", None)),
        check_vma=False,
    )
```

```python
import functools

import jax
import jax.numpy as jnp
from jax import lax
from jax.experimental import pallas as pl
from jax.experimental.pallas import tpu as pltpu
from jax.sharding import PartitionSpec as P

TOP = 8


def shifted(array, axis, by):
    count = lax.axis_size(axis)
    return lax.ppermute(array, axis, [(i, (i + by) % count) for i in range(count)])


def routing(expert_ids, gate_prob, experts, capacity):
    tok_count = expert_ids.shape[0]
    pick_count = expert_ids.shape[1]
    entry_count = tok_count * pick_count
    flat_ids = expert_ids.reshape(entry_count)
    one_hot = (flat_ids[:, None] == jnp.arange(experts, dtype=jnp.int32)[None, :]).astype(
        jnp.float32
    )
    entry_index = jnp.arange(entry_count, dtype=jnp.int32)
    strictly_lower = (entry_index[:, None] > entry_index[None, :]).astype(jnp.float32)
    earlier = jnp.dot(strictly_lower, one_hot, precision=lax.Precision.HIGHEST)
    slot_index = jnp.sum(earlier * one_hot, axis=1)
    slot_range = jnp.arange(capacity, dtype=jnp.int32).astype(jnp.float32)
    slot_hot = (slot_range[None, :] == slot_index[:, None]).astype(jnp.float32)
    placed = (one_hot[:, :, None] * slot_hot[:, None, :]).reshape(
        tok_count, pick_count, experts * capacity
    )
    select_mat = jnp.sum(placed, axis=1)
    weigh_mat = jnp.sum(placed * gate_prob[:, :, None], axis=1)
    return (select_mat, weigh_mat)


def dispatch(select_mat, values):
    moved = lax.dot_general(
        select_mat.astype(jnp.bfloat16),
        values,
        (((0,), (0,)), ((), ())),
        preferred_element_type=jnp.float32,
    )
    return moved.astype(jnp.bfloat16)


def weigh_rows(weigh_mat, grads):
    moved = lax.dot_general(
        weigh_mat,
        grads.astype(jnp.float32),
        (((0,), (0,)), ((), ())),
        precision=lax.Precision.HIGHEST,
        preferred_element_type=jnp.float32,
    )
    return moved.astype(jnp.bfloat16)


def collect(matrix, rows):
    return jnp.dot(matrix, rows.astype(jnp.float32), precision=lax.Precision.HIGHEST).astype(
        jnp.bfloat16
    )


def expert_forward(rows, gate_mat, up_mat, down_mat):
    gate_pre = jnp.dot(rows, gate_mat, preferred_element_type=jnp.float32)
    up_pre = jnp.dot(rows, up_mat, preferred_element_type=jnp.float32)
    hidden = (jax.nn.silu(gate_pre) * up_pre).astype(jnp.bfloat16)
    return jnp.dot(hidden, down_mat, preferred_element_type=jnp.float32).astype(jnp.bfloat16)


def expert_backward(rows, grad_rows, gate_mat, up_mat, down_mat):
    contract = (((1,), (1,)), ((), ()))
    gate_pre = jnp.dot(rows, gate_mat, preferred_element_type=jnp.float32)
    up_pre = jnp.dot(rows, up_mat, preferred_element_type=jnp.float32)
    grad_hidden = lax.dot_general(grad_rows, down_mat, contract, preferred_element_type=jnp.float32)
    sigma = jax.nn.sigmoid(gate_pre)
    grad_gate = (grad_hidden * up_pre * sigma * (1.0 + gate_pre * (1.0 - sigma))).astype(
        jnp.bfloat16
    )
    grad_up = (grad_hidden * gate_pre * sigma).astype(jnp.bfloat16)
    back = lax.dot_general(grad_gate, gate_mat, contract, preferred_element_type=jnp.float32)
    back = back + lax.dot_general(grad_up, up_mat, contract, preferred_element_type=jnp.float32)
    return back.astype(jnp.bfloat16)


def plain_body(fwd_acts, fwd_ids, fwd_prob, bwd_acts, bwd_ids, bwd_prob, grad_in, w_gate, w_up, w_down):
    experts = lax.axis_size("expert")
    tok_count = fwd_acts.shape[1]
    width = fwd_acts.shape[2]
    capacity = max(2, (tok_count * TOP + experts - 1) // experts)
    gate_mat = w_gate[0, 0]
    up_mat = w_up[0, 0]
    down_mat = w_down[0, 0]
    fwd_select, fwd_weigh = routing(fwd_ids[0], fwd_prob[0], experts, capacity)
    bwd_select, bwd_weigh = routing(bwd_ids[0], bwd_prob[0], experts, capacity)
    fwd_rows = dispatch(fwd_select, fwd_acts[0]).reshape(experts, capacity, width)
    bwd_rows = dispatch(bwd_select, bwd_acts[0]).reshape(experts, capacity, width)
    grad_rows = weigh_rows(bwd_weigh, grad_in[0]).reshape(experts, capacity, width)

    def backward_rows(received, received_grad):
        flat_grad = received_grad.reshape(-1, width)
        return expert_backward(
            received.reshape(-1, width), flat_grad, gate_mat, up_mat, down_mat
        ).reshape(received.shape)

    received = lax.all_to_all(fwd_rows, "expert", split_axis=0, concat_axis=0, tiled=True)
    fwd_back = lax.all_to_all(
        expert_forward(received.reshape(-1, width), gate_mat, up_mat, down_mat).reshape(
            received.shape
        ),
        "expert",
        split_axis=0,
        concat_axis=0,
        tiled=True,
    )
    received = (
        lax.all_to_all(bwd_rows, "expert", split_axis=0, concat_axis=0, tiled=True),
        lax.all_to_all(grad_rows, "expert", split_axis=0, concat_axis=0, tiled=True),
    )
    bwd_back = lax.all_to_all(
        backward_rows(received[0], received[1]), "expert", split_axis=0, concat_axis=0, tiled=True
    )
    fwd_result = collect(fwd_weigh, fwd_back.reshape(-1, width))
    bwd_result = collect(bwd_select, bwd_back.reshape(-1, width))
    fwd_out = shifted(fwd_result[None], "segment", 1)
    bwd_out = shifted(bwd_result[None], "segment", -1)
    return (fwd_out, bwd_out)


MESH = pl.DeviceIdType.MESH
LANES = 128
NT = (((1,), (1,)), ((), ()))
BWD, GRAD, FWD = 0, 1, 2


def moe_kernel(
    n,
    sections,
    chunks,
    bwd_ref,
    grad_ref,
    fwd_ref,
    fid_ref,
    fpr_ref,
    bid_ref,
    bpr_ref,
    wg_ref,
    wu_ref,
    wd_ref,
    fout_ref,
    bout_ref,
    gat,
    prob,
    xbuf,
    gbuf,
    wgate,
    wup,
    wdown,
    part,
    mid,
    own,
    ysend,
    yrecv,
    zsend,
    zrecv,
    local_sem,
    wlocal_sem,
    wsend_sem,
    wrecv_sem,
    az_send,
    az_recv,
    ay_send,
    ay_recv,
    ry_send,
    ry_recv,
    rz_send,
    rz_recv,
):
    far = n // 4
    tok, width = bwd_ref.shape
    hid = wd_ref.shape[0]
    rows = 2 * far * tok
    cw = width // chunks
    sec = lax.axis_index("segment")
    me = lax.axis_index("expert")
    core = lax.rem(me, 2)
    y = lax.rem(me // 2, 2)
    z = me // 4

    def place(zz, yy, cc):
        return (zz * 2 + yy) * 2 + cc

    partner = place(z, y, 1 - core)
    across = place(z, 1 - y, core)
    next_sec = lax.rem(sec + 1, sections)
    prev_sec = lax.rem(sec + sections - 1, sections)
    peers = [lax.rem(z + d, far) for d in range(1, far)]

    barrier = pltpu.get_barrier_semaphore()
    greeted = [(sec, partner), (sec, across)] + [(sec, place(p, y, core)) for p in peers]
    for other in [next_sec] if sections == 2 else [next_sec, prev_sec]:
        greeted += [(other, place(zz, y, core)) for zz in range(far)]
    for target in greeted:
        pl.semaphore_signal(barrier, inc=1, device_id=target, device_id_type=MESH)

    local = []
    for a, ref in ((BWD, bwd_ref), (GRAD, grad_ref), (FWD, fwd_ref)):
        local.append(pltpu.make_async_copy(ref, gat.at[a, 0, z], local_sem.at[a]))
    for cp in local:
        cp.start()
    wlocal = [
        pltpu.make_async_copy(ref, buf.at[0], wlocal_sem.at[k])
        for k, (ref, buf) in enumerate(((wg_ref, wgate), (wu_ref, wup), (wd_ref, wdown)))
    ]
    for cp in wlocal:
        cp.start()
    lanes = prob.shape[-1]
    line = lax.broadcasted_iota(jnp.int32, (lanes, tok), 0)
    table = jnp.zeros((lanes, tok), jnp.float32)
    for k in range(fid_ref.shape[0]):
        table += jnp.where(fid_ref[k : k + 1, :] == line, fpr_ref[k : k + 1, :], 0.0)
        table += jnp.where(bid_ref[k : k + 1, :] + n == line, bpr_ref[k : k + 1, :], 0.0)
    prob[0, z] = table.T

    pl.semaphore_wait(barrier, len(greeted))

    def view(a):
        return prob if a == 3 else gat.at[a]

    def remote(src, dst, send, recv, device):
        return pltpu.make_async_remote_copy(
            src_ref=src,
            dst_ref=dst,
            send_sem=send,
            recv_sem=recv,
            device_id=device,
            device_id_type=MESH,
        )

    def z_copy(a, src, zs, way):
        return remote(
            src,
            view(a).at[0, zs],
            az_send.at[a, way, zs],
            az_recv.at[a, zs],
            (sec, place(z + (1 - 2 * way), y, core)),
        )

    def y_copy(a, src, zs):
        return remote(src, view(a).at[1, zs], ay_send.at[a, zs], ay_recv.at[a, zs], (sec, across))

    started = []
    guarded = []

    def onward(a, src, zs, valid):
        for way, there in valid:
            cp = z_copy(a, src, zs, way)
            pl.when(there)(cp.start)
            guarded.append((there, cp))

    def send_own(a, ref):
        onward(a, ref, z, ((0, z + 1 < far), (1, z > 0)))
        cp = y_copy(a, ref, z)
        cp.start()
        started.append(cp)

    def relay(a, hops):
        for way in range(2):
            step = 1 - 2 * way
            zs = z - step * (hops + 1)
            here = jnp.logical_and(zs >= 0, zs < far)
            further = jnp.logical_and(here, z + 1 < far if way == 0 else z > 0)
            ref = view(a).at[0, zs]
            cp = y_copy(a, ref, zs)
            on = z_copy(a, ref, zs, way)

            @pl.when(here)
            def _():
                on.wait_recv()
                pl.when(further)(on.start)
                cp.start()

            guarded.append((here, cp))
            guarded.append((further, on))

    send_own(BWD, bwd_ref)
    send_own(GRAD, grad_ref)
    send_own(3, prob.at[0, z])
    for k, (w, buf) in enumerate(((wg_ref, wgate), (wu_ref, wup), (wd_ref, wdown))):
        cp = remote(w, buf.at[1], wsend_sem.at[k], wrecv_sem.at[k], (sec, partner))
        cp.start()
        started.append(cp)

    def arrive(a):
        for zs in range(far):
            ref = view(a).at[1, zs]
            remote(ref, ref, ay_send.at[a, zs], ay_recv.at[a, zs], (sec, across)).wait_recv()

    def flatten(a, dst):
        for b in range(far):
            both = []
            for q in (2 * b, 2 * b + 1):
                both.append(gat[a, q // far, q % far].astype(jnp.float32))
            dst[2 * b * tok : (2 * b + 2) * tok, :] = jnp.concatenate(both, axis=0).astype(
                jnp.bfloat16
            )

    def weight_of(base, slot):
        index = base + (me if slot == 0 else partner)
        full = prob[...].reshape(rows, lanes)
        at = lax.broadcasted_iota(jnp.int32, (rows, lanes), 1) == index
        return jnp.sum(jnp.where(at, full, 0.0), axis=1, keepdims=True)

    def partial_out(r, c, value):
        half = far * tok
        own[r, c] = value[:half]
        for zz in range(far):
            lo = half + zz * tok
            ysend[r, c, zz] = value[lo : lo + tok].astype(jnp.bfloat16)
        cp = remote(
            ysend.at[r, c], yrecv.at[r, c], ry_send.at[r, c], ry_recv.at[r, c], (sec, across)
        )
        cp.start()
        started.append(cp)

    def second_hop(r, section):
        for c in range(chunks):
            remote(
                ysend.at[r, c], yrecv.at[r, c], ry_send.at[r, c], ry_recv.at[r, c], (sec, across)
            ).wait_recv()
            for zz in range(far):
                total = own[r, c, zz * tok : (zz + 1) * tok] + yrecv[r, c, zz].astype(jnp.float32)
                zsend[r, c, zz] = total.astype(jnp.bfloat16)
            for zz in range(far):
                cp = remote(
                    zsend.at[r, c, zz],
                    zrecv.at[r, c, z],
                    rz_send.at[r, c, zz],
                    rz_recv.at[r, c, z],
                    (section, place(zz, y, core)),
                )
                cp.start()
                started.append(cp)

    def finish(r, section, out_ref):
        for c in range(chunks):
            total = None
            for zz in range(far):
                ref = zrecv.at[r, c, zz]
                remote(
                    ref, ref, rz_send.at[r, c, zz], rz_recv.at[r, c, zz], (section, me)
                ).wait_recv()
                got = zrecv[r, c, zz].astype(jnp.float32)
                total = got if total is None else total + got
            out_ref[:, c * cw : (c + 1) * cw] = total.astype(jnp.bfloat16)

    def mm(a, b):
        return jnp.dot(a, b, preferred_element_type=jnp.float32)

    def mm_t(a, b):
        return lax.dot_general(a, b, NT, preferred_element_type=jnp.float32)

    for hops in range(far - 1):
        if hops == far - 2:
            send_own(FWD, fwd_ref)
        for a in (BWD, GRAD, 3):
            relay(a, hops)
        if hops == far - 2:
            relay(FWD, 0)
    local[BWD].wait()
    arrive(BWD)
    flatten(BWD, xbuf)
    for slot in range(2):
        for k in range(3):
            if slot == 0:
                wlocal[k].wait()
            else:
                buf = (wgate, wup, wdown)[k].at[1]
                remote(buf, buf, wsend_sem.at[k], wrecv_sem.at[k], (sec, partner)).wait_recv()
        part[0] = mm(xbuf[...], wgate[slot])
        part[1] = mm(xbuf[...], wup[slot])
        if slot == 0:
            local[GRAD].wait()
            arrive(GRAD)
            arrive(3)
            flatten(GRAD, gbuf)
        grad_hidden = mm_t(gbuf[...], wdown[slot]) * weight_of(n, slot)
        gate_pre = part[0]
        sigma = jax.nn.sigmoid(gate_pre)
        mid[2 * slot] = (
            grad_hidden * part[1] * sigma * (1.0 + gate_pre * (1.0 - sigma))
        ).astype(jnp.bfloat16)
        mid[2 * slot + 1] = (grad_hidden * gate_pre * sigma).astype(jnp.bfloat16)
        if slot == 0:
            for hops in range(1, far - 1):
                relay(FWD, hops)
    for c in range(chunks):
        cols = slice(c * cw, (c + 1) * cw)
        value = mm_t(mid[0], wgate[0, cols, :])
        value += mm_t(mid[1], wup[0, cols, :])
        value += mm_t(mid[2], wgate[1, cols, :])
        value += mm_t(mid[3], wup[1, cols, :])
        partial_out(0, c, value)

    local[FWD].wait()
    arrive(FWD)
    flatten(FWD, xbuf)
    for slot in range(2):
        part[0] = mm(xbuf[...], wgate[slot])
        up_pre = mm(xbuf[...], wup[slot])
        gate_pre = part[0]
        hidden = gate_pre * jax.nn.sigmoid(gate_pre) * up_pre * weight_of(0, slot)
        mid[slot] = hidden.astype(jnp.bfloat16)
        if slot == 0:
            second_hop(0, prev_sec)
    for c in range(chunks):
        cols = slice(c * cw, (c + 1) * cw)
        value = mm(mid[0], wdown[0, :, cols])
        value += mm(mid[1], wdown[1, :, cols])
        partial_out(1, c, value)
    second_hop(1, next_sec)
    finish(0, prev_sec, bout_ref)
    finish(1, next_sec, fout_ref)
    for cp in started:
        cp.wait_send()
    for there, cp in guarded:
        pl.when(there)(cp.wait_send)


def fused_body(n, sections, chunks, *args):
    fwd_acts, fwd_ids, fwd_prob, bwd_acts, bwd_ids, bwd_prob, grad_in, w_gate, w_up, w_down = args
    tok, width = fwd_acts.shape[1:]
    hid = w_down.shape[2]
    far = n // 4
    rows = 2 * far * tok
    cw = width // chunks
    lanes = -(-2 * n // LANES) * LANES
    bf, f32 = jnp.bfloat16, jnp.float32
    dma = pltpu.SemaphoreType.DMA
    fwd_out, bwd_out = pl.pallas_call(
        functools.partial(moe_kernel, n, sections, chunks),
        out_shape=[jax.ShapeDtypeStruct((tok, width), bf)] * 2,
        in_specs=[pl.BlockSpec(memory_space=pl.ANY)] * 3
        + [pl.BlockSpec(memory_space=pltpu.VMEM)] * 4
        + [pl.BlockSpec(memory_space=pl.ANY)] * 3,
        out_specs=[pl.BlockSpec(memory_space=pltpu.VMEM)] * 2,
        scratch_shapes=[
            pltpu.VMEM((3, 2, far, tok, width), bf),
            pltpu.VMEM((2, far, tok, lanes), f32),
            pltpu.VMEM((rows, width), bf),
            pltpu.VMEM((rows, width), bf),
            pltpu.VMEM((2, width, hid), bf),
            pltpu.VMEM((2, width, hid), bf),
            pltpu.VMEM((2, hid, width), bf),
            pltpu.VMEM((2, rows, hid), f32),
            pltpu.VMEM((4, rows, hid), bf),
            pltpu.VMEM((2, chunks, far * tok, cw), f32),
            pltpu.VMEM((2, chunks, far, tok, cw), bf),
            pltpu.VMEM((2, chunks, far, tok, cw), bf),
            pltpu.VMEM((2, chunks, far, tok, cw), bf),
            pltpu.VMEM((2, chunks, far, tok, cw), bf),
            dma((3,)),
            dma((3,)),
            dma((3,)),
            dma((3,)),
            dma((4, 2, far)),
            dma((4, far)),
            dma((4, far)),
            dma((4, far)),
            dma((2, chunks)),
            dma((2, chunks)),
            dma((2, chunks, far)),
            dma((2, chunks, far)),
        ],
        compiler_params=pltpu.CompilerParams(
            collective_id=0, has_side_effects=True, vmem_limit_bytes=60 * 1024 * 1024
        ),
    )(
        bwd_acts[0],
        grad_in[0],
        fwd_acts[0],
        fwd_ids[0].T,
        fwd_prob[0].T,
        bwd_ids[0].T,
        bwd_prob[0].T,
        w_gate[0, 0],
        w_up[0, 0],
        w_down[0, 0],
    )
    return fwd_out[None], bwd_out[None]


def body(*args):
    n = lax.axis_size("expert")
    sections = lax.axis_size("segment")
    tok, width = args[0].shape[1:]
    gathered = n * tok * width * 2
    fits = n % 4 == 0 and n >= 8 and sections > 1 and tok % 8 == 0 and width % 512 == 0
    if not fits or gathered > 4 * 1024 * 1024:
        return plain_body(*args)
    return fused_body(n, sections, width // 512, *args)


def solution(mesh):
    return jax.shard_map(
        body,
        mesh=mesh,
        in_specs=(
            P("segment", "expert", None),
            P("segment", "expert", None),
            P("segment", "expert", None),
            P("segment", "expert", None),
            P("segment", "expert", None),
            P("segment", "expert", None),
            P("segment", "expert", None),
            P("segment", "expert", None, None),
            P("segment", "expert", None, None),
            P("segment", "expert", None, None),
        ),
        out_specs=(P("segment", "expert", None), P("segment", "expert", None)),
        check_vma=False,
    )
```

```python
import functools

import jax
import jax.numpy as jnp
from jax import lax
from jax.experimental import pallas as pl
from jax.experimental.pallas import tpu as pltpu
from jax.sharding import PartitionSpec as P

TOP = 8


def shifted(array, axis, by):
    count = lax.axis_size(axis)
    return lax.ppermute(array, axis, [(i, (i + by) % count) for i in range(count)])


def routing(expert_ids, gate_prob, experts, capacity):
    tok_count = expert_ids.shape[0]
    pick_count = expert_ids.shape[1]
    entry_count = tok_count * pick_count
    flat_ids = expert_ids.reshape(entry_count)
    one_hot = (flat_ids[:, None] == jnp.arange(experts, dtype=jnp.int32)[None, :]).astype(
        jnp.float32
    )
    entry_index = jnp.arange(entry_count, dtype=jnp.int32)
    strictly_lower = (entry_index[:, None] > entry_index[None, :]).astype(jnp.float32)
    earlier = jnp.dot(strictly_lower, one_hot, precision=lax.Precision.HIGHEST)
    slot_index = jnp.sum(earlier * one_hot, axis=1)
    slot_range = jnp.arange(capacity, dtype=jnp.int32).astype(jnp.float32)
    slot_hot = (slot_range[None, :] == slot_index[:, None]).astype(jnp.float32)
    placed = (one_hot[:, :, None] * slot_hot[:, None, :]).reshape(
        tok_count, pick_count, experts * capacity
    )
    select_mat = jnp.sum(placed, axis=1)
    weigh_mat = jnp.sum(placed * gate_prob[:, :, None], axis=1)
    return (select_mat, weigh_mat)


def dispatch(select_mat, values):
    moved = lax.dot_general(
        select_mat.astype(jnp.bfloat16),
        values,
        (((0,), (0,)), ((), ())),
        preferred_element_type=jnp.float32,
    )
    return moved.astype(jnp.bfloat16)


def weigh_rows(weigh_mat, grads):
    moved = lax.dot_general(
        weigh_mat,
        grads.astype(jnp.float32),
        (((0,), (0,)), ((), ())),
        precision=lax.Precision.HIGHEST,
        preferred_element_type=jnp.float32,
    )
    return moved.astype(jnp.bfloat16)


def collect(matrix, rows):
    return jnp.dot(matrix, rows.astype(jnp.float32), precision=lax.Precision.HIGHEST).astype(
        jnp.bfloat16
    )


def expert_forward(rows, gate_mat, up_mat, down_mat):
    gate_pre = jnp.dot(rows, gate_mat, preferred_element_type=jnp.float32)
    up_pre = jnp.dot(rows, up_mat, preferred_element_type=jnp.float32)
    hidden = (jax.nn.silu(gate_pre) * up_pre).astype(jnp.bfloat16)
    return jnp.dot(hidden, down_mat, preferred_element_type=jnp.float32).astype(jnp.bfloat16)


def expert_backward(rows, grad_rows, gate_mat, up_mat, down_mat):
    contract = (((1,), (1,)), ((), ()))
    gate_pre = jnp.dot(rows, gate_mat, preferred_element_type=jnp.float32)
    up_pre = jnp.dot(rows, up_mat, preferred_element_type=jnp.float32)
    grad_hidden = lax.dot_general(grad_rows, down_mat, contract, preferred_element_type=jnp.float32)
    sigma = jax.nn.sigmoid(gate_pre)
    grad_gate = (grad_hidden * up_pre * sigma * (1.0 + gate_pre * (1.0 - sigma))).astype(
        jnp.bfloat16
    )
    grad_up = (grad_hidden * gate_pre * sigma).astype(jnp.bfloat16)
    back = lax.dot_general(grad_gate, gate_mat, contract, preferred_element_type=jnp.float32)
    back = back + lax.dot_general(grad_up, up_mat, contract, preferred_element_type=jnp.float32)
    return back.astype(jnp.bfloat16)


def plain_body(fwd_acts, fwd_ids, fwd_prob, bwd_acts, bwd_ids, bwd_prob, grad_in, w_gate, w_up, w_down):
    experts = lax.axis_size("expert")
    tok_count = fwd_acts.shape[1]
    width = fwd_acts.shape[2]
    capacity = max(2, (tok_count * TOP + experts - 1) // experts)
    gate_mat = w_gate[0, 0]
    up_mat = w_up[0, 0]
    down_mat = w_down[0, 0]
    fwd_select, fwd_weigh = routing(fwd_ids[0], fwd_prob[0], experts, capacity)
    bwd_select, bwd_weigh = routing(bwd_ids[0], bwd_prob[0], experts, capacity)
    fwd_rows = dispatch(fwd_select, fwd_acts[0]).reshape(experts, capacity, width)
    bwd_rows = dispatch(bwd_select, bwd_acts[0]).reshape(experts, capacity, width)
    grad_rows = weigh_rows(bwd_weigh, grad_in[0]).reshape(experts, capacity, width)

    def backward_rows(received, received_grad):
        flat_grad = received_grad.reshape(-1, width)
        return expert_backward(
            received.reshape(-1, width), flat_grad, gate_mat, up_mat, down_mat
        ).reshape(received.shape)

    received = lax.all_to_all(fwd_rows, "expert", split_axis=0, concat_axis=0, tiled=True)
    fwd_back = lax.all_to_all(
        expert_forward(received.reshape(-1, width), gate_mat, up_mat, down_mat).reshape(
            received.shape
        ),
        "expert",
        split_axis=0,
        concat_axis=0,
        tiled=True,
    )
    received = (
        lax.all_to_all(bwd_rows, "expert", split_axis=0, concat_axis=0, tiled=True),
        lax.all_to_all(grad_rows, "expert", split_axis=0, concat_axis=0, tiled=True),
    )
    bwd_back = lax.all_to_all(
        backward_rows(received[0], received[1]), "expert", split_axis=0, concat_axis=0, tiled=True
    )
    fwd_result = collect(fwd_weigh, fwd_back.reshape(-1, width))
    bwd_result = collect(bwd_select, bwd_back.reshape(-1, width))
    fwd_out = shifted(fwd_result[None], "segment", 1)
    bwd_out = shifted(bwd_result[None], "segment", -1)
    return (fwd_out, bwd_out)


MESH = pl.DeviceIdType.MESH
LANES = 128
NT = (((1,), (1,)), ((), ()))
BWD, GRAD, FWD = 0, 1, 2


def moe_kernel(
    n,
    sections,
    chunks,
    bwd_ref,
    grad_ref,
    fwd_ref,
    fid_ref,
    fpr_ref,
    bid_ref,
    bpr_ref,
    wg_ref,
    wu_ref,
    wd_ref,
    fout_ref,
    bout_ref,
    gat,
    prob,
    xbuf,
    gbuf,
    wgate,
    wup,
    wdown,
    part,
    mid,
    own,
    ysend,
    yrecv,
    zsend,
    zrecv,
    local_sem,
    wlocal_sem,
    wsend_sem,
    wrecv_sem,
    az_send,
    az_recv,
    ay_send,
    ay_recv,
    bz_send,
    bz_recv,
    by_sem,
    ry_send,
    ry_recv,
    rz_send,
    rz_recv,
):
    far = n // 4
    tok, width = bwd_ref.shape
    hid = wd_ref.shape[0]
    rows = 2 * far * tok
    cw = width // chunks
    sec = lax.axis_index("segment")
    me = lax.axis_index("expert")
    core = lax.rem(me, 2)
    y = lax.rem(me // 2, 2)
    z = me // 4

    def place(zz, yy, cc):
        return (zz * 2 + yy) * 2 + cc

    partner = place(z, y, 1 - core)
    across = place(z, 1 - y, core)
    next_sec = lax.rem(sec + 1, sections)
    prev_sec = lax.rem(sec + sections - 1, sections)
    peers = [lax.rem(z + d, far) for d in range(1, far)]

    barrier = pltpu.get_barrier_semaphore()
    greeted = [(sec, partner), (sec, across)] + [(sec, place(p, y, core)) for p in peers]
    for other in [next_sec] if sections == 2 else [next_sec, prev_sec]:
        greeted += [(other, place(zz, y, core)) for zz in range(far)]
    for target in greeted:
        pl.semaphore_signal(barrier, inc=1, device_id=target, device_id_type=MESH)

    local = []
    for a, ref in ((BWD, bwd_ref), (GRAD, grad_ref), (FWD, fwd_ref)):
        local.append(pltpu.make_async_copy(ref, gat.at[a, 0, z], local_sem.at[a]))
    for cp in local:
        cp.start()
    wlocal = [
        pltpu.make_async_copy(ref, buf.at[0], wlocal_sem.at[k])
        for k, (ref, buf) in enumerate(((wg_ref, wgate), (wu_ref, wup), (wd_ref, wdown)))
    ]
    for cp in wlocal:
        cp.start()
    lanes = prob.shape[-1]
    line = lax.broadcasted_iota(jnp.int32, (lanes, tok), 0)
    table = jnp.zeros((lanes, tok), jnp.float32)
    for k in range(fid_ref.shape[0]):
        table += jnp.where(fid_ref[k : k + 1, :] == line, fpr_ref[k : k + 1, :], 0.0)
        table += jnp.where(bid_ref[k : k + 1, :] + n == line, bpr_ref[k : k + 1, :], 0.0)
    prob[0, z] = table.T

    pl.semaphore_wait(barrier, len(greeted))

    cut = width // 2

    def block(a, row, zs):
        if a == 3:
            return prob.at[row, zs]
        if a == FWD:
            return gat.at[a, row, zs, :, pl.ds(0, cut)]
        return gat.at[a, row, zs]

    def late(row, zs):
        return gat.at[FWD, row, zs, :, pl.ds(cut, width - cut)]

    def remote(src, dst, send, recv, device):
        return pltpu.make_async_remote_copy(
            src_ref=src,
            dst_ref=dst,
            send_sem=send,
            recv_sem=recv,
            device_id=device,
            device_id_type=MESH,
        )

    def z_copy(a, src, zs, way):
        return remote(
            src,
            block(a, 0, zs),
            az_send.at[a, way, zs],
            az_recv.at[a, zs],
            (sec, place(z + (1 - 2 * way), y, core)),
        )

    def y_copy(a, src, zs):
        return remote(src, block(a, 1, zs), ay_send.at[a, zs], ay_recv.at[a, zs], (sec, across))

    started = []
    guarded = []

    def onward(a, src, zs, valid):
        for way, there in valid:
            cp = z_copy(a, src, zs, way)
            pl.when(there)(cp.start)
            guarded.append((there, cp))

    def send_own(a, ref):
        onward(a, ref, z, ((0, z + 1 < far), (1, z > 0)))
        cp = y_copy(a, ref, z)
        cp.start()
        started.append(cp)

    def relay(a, hops):
        for way in range(2):
            step = 1 - 2 * way
            zs = z - step * (hops + 1)
            here = jnp.logical_and(zs >= 0, zs < far)
            further = jnp.logical_and(here, z + 1 < far if way == 0 else z > 0)
            ref = block(a, 0, zs)
            cp = y_copy(a, ref, zs)
            on = z_copy(a, ref, zs, way)

            @pl.when(here)
            def _():
                on.wait_recv()
                pl.when(further)(on.start)
                cp.start()

            guarded.append((here, cp))
            guarded.append((further, on))

    def late_copy(row, src, zs, way):
        return remote(
            src,
            late(row, zs),
            bz_send.at[row, way, zs],
            bz_recv.at[row, zs],
            (sec, place(z + (1 - 2 * way), y, core)),
        )

    def late_send(row, src):
        for way, there in ((0, z + 1 < far), (1, z > 0)):
            cp = late_copy(row, src, z, way)
            pl.when(there)(cp.start)
            guarded.append((there, cp))

    def late_relay(row, hops):
        for way in range(2):
            zs = z - (1 - 2 * way) * (hops + 1)
            here = jnp.logical_and(zs >= 0, zs < far)
            further = jnp.logical_and(here, z + 1 < far if way == 0 else z > 0)
            on = late_copy(row, late(row, zs), zs, way)

            @pl.when(here)
            def _():
                on.wait_recv()
                pl.when(further)(on.start)

            guarded.append((further, on))

    fwd_late = fwd_ref.at[:, pl.ds(cut, width - cut)]
    late_across = remote(fwd_late, late(1, z), by_sem.at[0], by_sem.at[1], (sec, across))
    send_own(BWD, bwd_ref)
    send_own(GRAD, grad_ref)
    late_across.start()
    started.append(late_across)
    send_own(3, prob.at[0, z])
    for k, (w, buf) in enumerate(((wg_ref, wgate), (wu_ref, wup), (wd_ref, wdown))):
        cp = remote(w, buf.at[1], wsend_sem.at[k], wrecv_sem.at[k], (sec, partner))
        cp.start()
        started.append(cp)

    def arrive(a):
        for zs in range(far):
            ref = block(a, 1, zs)
            remote(ref, ref, ay_send.at[a, zs], ay_recv.at[a, zs], (sec, across)).wait_recv()

    def flatten(a, dst):
        for b in range(far):
            both = []
            for q in (2 * b, 2 * b + 1):
                both.append(gat[a, q // far, q % far].astype(jnp.float32))
            dst[2 * b * tok : (2 * b + 2) * tok, :] = jnp.concatenate(both, axis=0).astype(
                jnp.bfloat16
            )

    def weight_of(base, slot):
        index = base + (me if slot == 0 else partner)
        full = prob[...].reshape(rows, lanes)
        at = lax.broadcasted_iota(jnp.int32, (rows, lanes), 1) == index
        return jnp.sum(jnp.where(at, full, 0.0), axis=1, keepdims=True)

    def partial_out(r, c, value):
        half = far * tok
        own[r, c] = value[:half]
        for zz in range(far):
            lo = half + zz * tok
            ysend[r, c, zz] = value[lo : lo + tok].astype(jnp.bfloat16)
        cp = remote(
            ysend.at[r, c], yrecv.at[r, c], ry_send.at[r, c], ry_recv.at[r, c], (sec, across)
        )
        cp.start()
        started.append(cp)

    def second_hop(r, section, which):
        for c in which:
            remote(
                ysend.at[r, c], yrecv.at[r, c], ry_send.at[r, c], ry_recv.at[r, c], (sec, across)
            ).wait_recv()
            for zz in range(far):
                total = own[r, c, zz * tok : (zz + 1) * tok] + yrecv[r, c, zz].astype(jnp.float32)
                zsend[r, c, zz] = total.astype(jnp.bfloat16)
            for zz in range(far):
                cp = remote(
                    zsend.at[r, c, zz],
                    zrecv.at[r, c, z],
                    rz_send.at[r, c, zz],
                    rz_recv.at[r, c, z],
                    (section, place(zz, y, core)),
                )
                cp.start()
                started.append(cp)

    def finish(r, section, out_ref):
        for c in range(chunks):
            total = None
            for zz in range(far):
                ref = zrecv.at[r, c, zz]
                remote(
                    ref, ref, rz_send.at[r, c, zz], rz_recv.at[r, c, zz], (section, me)
                ).wait_recv()
                got = zrecv[r, c, zz].astype(jnp.float32)
                total = got if total is None else total + got
            out_ref[:, c * cw : (c + 1) * cw] = total.astype(jnp.bfloat16)

    def mm(a, b):
        return jnp.dot(a, b, preferred_element_type=jnp.float32)

    def mm_t(a, b):
        return lax.dot_general(a, b, NT, preferred_element_type=jnp.float32)

    for hops in range(far - 1):
        if hops == far - 2:
            send_own(FWD, fwd_ref.at[:, pl.ds(0, cut)])
            late_send(0, fwd_late)
            late_across.wait_recv()
            late_send(1, late(1, z))
        for a in (BWD, GRAD, 3):
            relay(a, hops)
        if hops == far - 2:
            relay(FWD, 0)
            late_relay(0, 0)
            late_relay(1, 0)
    local[BWD].wait()
    arrive(BWD)
    flatten(BWD, xbuf)
    for slot in range(2):
        for k in range(3):
            if slot == 0:
                wlocal[k].wait()
            else:
                buf = (wgate, wup, wdown)[k].at[1]
                remote(buf, buf, wsend_sem.at[k], wrecv_sem.at[k], (sec, partner)).wait_recv()
        part[0] = mm(xbuf[...], wgate[slot])
        part[1] = mm(xbuf[...], wup[slot])
        if slot == 0:
            local[GRAD].wait()
            arrive(GRAD)
            arrive(3)
            flatten(GRAD, gbuf)
        grad_hidden = mm_t(gbuf[...], wdown[slot]) * weight_of(n, slot)
        gate_pre = part[0]
        sigma = jax.nn.sigmoid(gate_pre)
        mid[2 * slot] = (
            grad_hidden * part[1] * sigma * (1.0 + gate_pre * (1.0 - sigma))
        ).astype(jnp.bfloat16)
        mid[2 * slot + 1] = (grad_hidden * gate_pre * sigma).astype(jnp.bfloat16)
        for hops in range(1, far - 2) if slot == 0 else range(max(1, far - 2), far - 1):
            relay(FWD, hops)
            late_relay(0, hops)
            late_relay(1, hops)
    for c in range(chunks):
        cols = slice(c * cw, (c + 1) * cw)
        value = mm_t(mid[0], wgate[0, cols, :])
        value += mm_t(mid[1], wup[0, cols, :])
        value += mm_t(mid[2], wgate[1, cols, :])
        value += mm_t(mid[3], wup[1, cols, :])
        partial_out(0, c, value)

    local[FWD].wait()
    arrive(FWD)
    flatten(FWD, xbuf)
    for slot in range(2):
        part[0] = mm(xbuf[...], wgate[slot])
        up_pre = mm(xbuf[...], wup[slot])
        gate_pre = part[0]
        hidden = gate_pre * jax.nn.sigmoid(gate_pre) * up_pre * weight_of(0, slot)
        mid[slot] = hidden.astype(jnp.bfloat16)
    for c in range(chunks):
        cols = slice(c * cw, (c + 1) * cw)
        value = mm(mid[0], wdown[0, :, cols])
        value += mm(mid[1], wdown[1, :, cols])
        partial_out(1, c, value)
        second_hop(0, prev_sec, [c])
    second_hop(1, next_sec, range(chunks))
    finish(0, prev_sec, bout_ref)
    finish(1, next_sec, fout_ref)
    for cp in started:
        cp.wait_send()
    for there, cp in guarded:
        pl.when(there)(cp.wait_send)


def fused_body(n, sections, chunks, *args):
    fwd_acts, fwd_ids, fwd_prob, bwd_acts, bwd_ids, bwd_prob, grad_in, w_gate, w_up, w_down = args
    tok, width = fwd_acts.shape[1:]
    hid = w_down.shape[2]
    far = n // 4
    rows = 2 * far * tok
    cw = width // chunks
    lanes = -(-2 * n // LANES) * LANES
    bf, f32 = jnp.bfloat16, jnp.float32
    dma = pltpu.SemaphoreType.DMA
    fwd_out, bwd_out = pl.pallas_call(
        functools.partial(moe_kernel, n, sections, chunks),
        out_shape=[jax.ShapeDtypeStruct((tok, width), bf)] * 2,
        in_specs=[pl.BlockSpec(memory_space=pl.ANY)] * 3
        + [pl.BlockSpec(memory_space=pltpu.VMEM)] * 4
        + [pl.BlockSpec(memory_space=pl.ANY)] * 3,
        out_specs=[pl.BlockSpec(memory_space=pltpu.VMEM)] * 2,
        scratch_shapes=[
            pltpu.VMEM((3, 2, far, tok, width), bf),
            pltpu.VMEM((2, far, tok, lanes), f32),
            pltpu.VMEM((rows, width), bf),
            pltpu.VMEM((rows, width), bf),
            pltpu.VMEM((2, width, hid), bf),
            pltpu.VMEM((2, width, hid), bf),
            pltpu.VMEM((2, hid, width), bf),
            pltpu.VMEM((2, rows, hid), f32),
            pltpu.VMEM((4, rows, hid), bf),
            pltpu.VMEM((2, chunks, far * tok, cw), f32),
            pltpu.VMEM((2, chunks, far, tok, cw), bf),
            pltpu.VMEM((2, chunks, far, tok, cw), bf),
            pltpu.VMEM((2, chunks, far, tok, cw), bf),
            pltpu.VMEM((2, chunks, far, tok, cw), bf),
            dma((3,)),
            dma((3,)),
            dma((3,)),
            dma((3,)),
            dma((4, 2, far)),
            dma((4, far)),
            dma((4, far)),
            dma((4, far)),
            dma((2, 2, far)),
            dma((2, far)),
            dma((2,)),
            dma((2, chunks)),
            dma((2, chunks)),
            dma((2, chunks, far)),
            dma((2, chunks, far)),
        ],
        compiler_params=pltpu.CompilerParams(
            collective_id=0, has_side_effects=True, vmem_limit_bytes=60 * 1024 * 1024
        ),
    )(
        bwd_acts[0],
        grad_in[0],
        fwd_acts[0],
        fwd_ids[0].T,
        fwd_prob[0].T,
        bwd_ids[0].T,
        bwd_prob[0].T,
        w_gate[0, 0],
        w_up[0, 0],
        w_down[0, 0],
    )
    return fwd_out[None], bwd_out[None]


def body(*args):
    n = lax.axis_size("expert")
    sections = lax.axis_size("segment")
    tok, width = args[0].shape[1:]
    gathered = n * tok * width * 2
    fits = n % 4 == 0 and n >= 8 and sections > 1 and tok % 8 == 0 and width % 512 == 0
    if not fits or gathered > 4 * 1024 * 1024:
        return plain_body(*args)
    return fused_body(n, sections, width // 512, *args)


def solution(mesh):
    return jax.shard_map(
        body,
        mesh=mesh,
        in_specs=(
            P("segment", "expert", None),
            P("segment", "expert", None),
            P("segment", "expert", None),
            P("segment", "expert", None),
            P("segment", "expert", None),
            P("segment", "expert", None),
            P("segment", "expert", None),
            P("segment", "expert", None, None),
            P("segment", "expert", None, None),
            P("segment", "expert", None, None),
        ),
        out_specs=(P("segment", "expert", None), P("segment", "expert", None)),
        check_vma=False,
    )
```
